32 devices in a mesh: field: 2 (over x), expo: 8 (over z, y), sky: 2 (over core).
Axes of the slice: x: 2, y: 2, z: 4, core: 2. Of those that a mesh axis runs over, the one named last changes fastest.
Arguments:
- science: float32 [64, 64, 512], P(('field', 'expo'), 'sky'), parts along dimension 0, may hold values from -6 to 6
- inv_variance: float32 [64, 64, 512], P(('field', 'expo'), 'sky'), parts along dimension 0, may hold values from 0.25 to 4
- pixel_masks: int32 [64, 64, 512], P(('field', 'expo'), 'sky'), parts along dimension 0, may hold values 0 or 1
- point_spread: float32 [64, 5, 5], P(('field', 'expo')), parts along dimension 0, may hold values from 0.02 to 0.1
- tile_offset: int32 [8, 32], P(None, 'expo'), may hold values from 0 to 1
- column_shift: int32 [8, 32], P(None, 'expo'), may hold values from -128 to 128
- trail_kernel: float32 [8, 3, 3], P('expo'), may hold values from 0.1 to 1
Outputs:
- likelihood: float32 [16, 64, 512], P(('field', 'expo'), 'sky'), parts along dimension 0
The draws below stay inside these ranges and needn't reach their ends.
There are 2 independent parts, one for each index of `field`. The reference program is written for one: setup_inputs(seed, part) draws one part's arguments, and reference() takes and returns one part's arrays. A program takes and returns all parts, laid end to end along the dimension named above; an argument that names none is the same for every part. Nothing has to cross between parts.
All inputs are finite; a program needn't handle non-finite values. No bound on the sum of `pixel_masks` on one device may be relied on, other than what follows from the above.
Results may differ from the reference program's by a relative error of at most 0.0003.
Values sent between devices are 32-bit elements; how exact they have to be, the bound alone decides.
A program may use at most 128 MiB of HBM per device.

```python
import math
import jax
import jax.numpy as jnp
from jax import lax

ROWS_DEV = 32
W = 512
MAX_SHIFT = 128
E = 32
V = 8
H = 64


def plant(values, key, least, high):
    place = [jax.random.randint(jax.random.fold_in(key, axis), (), 0, length) for axis, length in enumerate(values.shape)]
    widest = values.shape.index(max(values.shape))
    beside = place[:widest] + [(place[widest] + 1) % values.shape[widest]] + place[widest + 1:]
    return values.at[tuple(place)].set(least).at[tuple(beside)].set(high)


def block_scale(rng, shape, cuts, smallest, top_value):
    level, own = 1.0, jax.random.fold_in(rng, 6)
    for position, blocks in cuts:
        steps = jnp.exp(jax.random.uniform(jax.random.fold_in(own, position), (blocks,), jnp.float32, smallest / len(cuts), top_value / len(cuts)))
        level = level * jnp.repeat(steps, shape[position] // blocks).reshape([-1 if axis == position else 1 for axis in range(len(shape))])
    return level


def gaussian(rng, extent, deviation, reach, cuts=(), kind=jnp.bfloat16):
    drawn = deviation * jax.random.normal(rng, extent, jnp.float32)
    if cuts:
        drawn = drawn * block_scale(rng, extent, cuts, -0.22, 0.18)
    return jnp.clip(drawn, -reach, reach).astype(kind)


def setup_inputs(seed: int = 0, part: int = 0) -> dict:
    key_list = jax.random.split(jax.random.key(seed), 8)
    part_keys = jax.random.split(jax.random.fold_in(key_list[7], part), 8)
    science = gaussian(part_keys[0], (E, H, W), 1.0, 6.0, ((0, 8), (1, 2)), jnp.float32)
    inv_variance = jnp.clip(jnp.exp(math.log(4.0) - 2.7725887 * jax.random.uniform(part_keys[1], (E, H, W), jnp.float32) ** block_scale(part_keys[1], (E, H, W), ((0, 8), (1, 2)), -0.2, 0.2)), 0.25, 4.0)
    pixel_masks = plant((jax.random.randint(part_keys[2], (E, H, W), 0, 8) < 7).astype(jnp.int32), jax.random.fold_in(part_keys[2], 1), 0, 1)
    point_spread = jnp.clip(0.02 + 0.08 * jax.random.uniform(part_keys[3], (E, 5, 5), jnp.float32) ** block_scale(part_keys[3], (E, 5, 5), ((0, 8),), -0.2, 0.2), 0.02, 0.1)
    tile_offset = plant(jax.random.randint(key_list[4], (V, E), 0, 2), jax.random.fold_in(key_list[4], 1), 0, 1).astype(jnp.int32)
    column_shift = plant(jax.random.randint(key_list[5], (V, E), 0 - MAX_SHIFT, MAX_SHIFT + 1), jax.random.fold_in(key_list[5], 1), 0 - MAX_SHIFT, MAX_SHIFT).astype(jnp.int32)
    trail_kernel = jnp.clip(0.1 + 0.9 * jax.random.uniform(key_list[6], (V, 3, 3), jnp.float32) ** block_scale(key_list[6], (V, 3, 3), ((0, 8),), -0.2, 0.2), 0.1, 1.0)
    return {"science": science, "inv_variance": inv_variance, "pixel_masks": pixel_masks, "point_spread": point_spread, "tile_offset": tile_offset, "column_shift": column_shift, "trail_kernel": trail_kernel}


def filter_taps(padded, kernel, row_count, column_count):
    taps = kernel.shape[-1]
    running = jnp.zeros(padded.shape[:-2] + (row_count, column_count), jnp.float32)
    for row_tap in range(taps):
        for column_tap in range(taps):
            running = running + kernel[:, row_tap, column_tap, None, None] * padded[..., row_tap:row_tap + row_count, column_tap:column_tap + column_count]
    return running

def shift_columns(wide, column_shifts, column_count):
    margin = (wide.shape[-1] - column_count) // 2

    def single(single_image, pixel_shift):
        return lax.dynamic_slice_in_dim(single_image, (margin - pixel_shift).astype(jnp.int32), column_count, 2)
    return jax.vmap(single, in_axes=(1, 0), out_axes=1)(wide, column_shifts)

def reference(science, inv_variance, pixel_masks, point_spread, tile_offset, column_shift, trail_kernel):
    row_count = science.shape[1]
    column_count = science.shape[2]
    weighted = inv_variance * pixel_masks.astype(jnp.float32)
    signal = science * weighted
    psi_images = filter_taps(jnp.pad(signal, ((0, 0), (2, 2), (2, 2))), point_spread, row_count, column_count)
    phi_images = filter_taps(jnp.pad(weighted, ((0, 0), (2, 2), (2, 2))), point_spread * point_spread, row_count, column_count)
    filtered = jnp.stack([psi_images, phi_images])
    rolled = jnp.roll(filtered, -ROWS_DEV, axis=2)
    padding = ((0, 0), (0, 0), (0, 0), (MAX_SHIFT, MAX_SHIFT))
    own_wide = jnp.pad(filtered, padding)
    rolled_wide = jnp.pad(rolled, padding)

    def stack_velocity(inputs):
        offsets, column_shifts = inputs
        source_wide = jnp.where(offsets[None, :, None, None] == 1, rolled_wide, own_wide)
        return lax.optimization_barrier(jnp.sum(shift_columns(source_wide, column_shifts, column_count), axis=1))
    stacks = lax.map(stack_velocity, (tile_offset, column_shift))
    rimmed = jnp.pad(stacks, ((0, 0), (0, 0), (1, 1), (1, 1)))
    psi_trail = filter_taps(rimmed[:, 0], trail_kernel, row_count, column_count)
    phi_trail = filter_taps(rimmed[:, 1], trail_kernel * trail_kernel, row_count, column_count)
    return psi_trail / jnp.sqrt(phi_trail + 1.0)
```

```python
import functools

import jax
import jax.numpy as jnp
from jax import lax
from jax.experimental import pallas as pl
from jax.experimental.pallas import tpu as pltpu
from jax.sharding import PartitionSpec as P

LANES = 128
SUB = 8
MESH = pl.DeviceIdType.MESH


def filter_rows(load, weights, taps, wide):
    sums = [None] * taps
    for a in range(taps):
        x = load(a)
        for b in range(taps):
            term = weights[a][b] * x
            sums[b] = term if sums[b] is None else sums[b] + term
    mid = taps // 2
    total = sums[mid]
    for b in range(taps):
        if b != mid:
            total = total + pltpu.roll(sums[b], (mid - b) % wide, 1)
    return total


def kernel(
    dims,
    sci, iv, msk, ps, off, shf, tk, out,
    sci_v, iv_v, msk_v, image, other, filt, part_stack,
    recv_ya, recv_yb, recv_a, recv_b, stack, trail, trail_in,
    in_sem, sky_s, sky_r, ya_s, ya_r, yb_s, yb_r, ring_s, ring_r, end_s, end_r,
):
    E, R, W, Y, Z = dims
    H = Z // 2
    taps = ps.shape[1]
    wide = W + LANES
    half_rows = R // 2
    tiles = W // LANES
    c = lax.axis_index("sky")
    me = lax.axis_index("expo")
    y = lax.rem(me, Y)
    z = me // Y
    sky = {"sky": 1 - c}
    y_peer = {"expo": z * Y + (Y - 1 - y)}
    z_peer = [
        {"expo": lax.rem(z + 1, Z) * Y + y},
        {"expo": lax.rem(z + Z - 1, Z) * Y + y},
    ]

    loads = []
    for e in range(E):
        trio = [
            pltpu.make_async_copy(src.at[e], dst.at[e], in_sem.at[n, e])
            for n, (src, dst) in enumerate(((iv, iv_v), (msk, msk_v), (sci, sci_v)))
        ]
        for copy in trio:
            copy.start()
        loads.append(trio)

    barrier = pltpu.get_barrier_semaphore()
    greeted = [sky] + ([y_peer] if Y > 1 else []) + (z_peer if Z > 1 else [])
    for peer in greeted:
        pl.semaphore_signal(barrier, inc=1, device_id=peer, device_id_type=MESH)

    top = 2 * R + SUB
    for e in range(E):
        image[e, 0:SUB, :] = jnp.zeros((SUB, wide), jnp.float32)
        image[e, top : top + SUB, :] = jnp.zeros((SUB, wide), jnp.float32)
        image[e, SUB:top, W:wide] = jnp.zeros((2 * R, LANES), jnp.float32)
        for t in range(2):
            for m in (0, tiles + 1, tiles + 2):
                filt[e, t, m] = jnp.zeros((R, LANES), jnp.float32)
    stack[0:SUB, :] = jnp.zeros((SUB, wide), jnp.float32)
    stack[top : top + SUB, :] = jnp.zeros((SUB, wide), jnp.float32)
    stack[SUB:top, W:wide] = jnp.zeros((2 * R, LANES), jnp.float32)

    own_rows = pl.ds(pl.multiple_of(SUB + R * c, SUB), R)

    def sky_copy(e):
        return pltpu.make_async_remote_copy(
            src_ref=other.at[e],
            dst_ref=image.at[e, own_rows, pl.ds(0, W)],
            send_sem=sky_s.at[e],
            recv_sem=sky_r.at[e],
            device_id=sky,
            device_id_type=MESH,
        )

    for e in range(E):
        for copy in loads[e]:
            copy.wait()
        w = iv_v[e] * msk_v[e].astype(jnp.float32)
        s = sci_v[e] * w
        image[e, own_rows, 0:W] = jnp.where(c == 0, s, w)
        other[e] = jnp.where(c == 0, w, s)
        if e == 0:
            pl.semaphore_wait(barrier, len(greeted))
        sky_copy(e).start()

    def power(value):
        return jnp.where(c == 0, value, value * value)

    def filter_one(e, carry):
        weights = [[power(ps[e, a, b]) for b in range(taps)] for a in range(taps)]
        sky_copy(e).wait_recv()
        for i in range(2 * R // SUB):
            def load(a):
                start = SUB * (i + 1) + a - taps // 2
                return image[e, start : start + SUB, :]

            total = filter_rows(load, weights, taps, wide)
            t, low = divmod(SUB * i, R)
            for k in range(tiles):
                filt[e, t, k + 1, low : low + SUB, :] = total[:, k * LANES : (k + 1) * LANES]
        return carry

    lax.fori_loop(0, E, filter_one, 0)

    lane = lax.broadcasted_iota(jnp.int32, (R, LANES), 1)

    def stack_group(zd):
        def one(j, carry):
            yy = j // 2
            t = lax.rem(j, 2)
            v = zd * Y + yy
            sums = [None] * tiles
            for e in range(E):
                o = LANES - shf[v, e]
                q = o // LANES
                r = o - q * LANES
                near = lane < LANES - r
                o_row = off[v, e]
                source = t + o_row - 2 * t * o_row
                turned = [pltpu.roll(filt[e, source, q + m], LANES - r, 1) for m in range(tiles + 1)]
                for k in range(tiles):
                    got = jnp.where(near, turned[k], turned[k + 1])
                    sums[k] = got if sums[k] is None else sums[k] + got
            for k in range(tiles):
                for p in range(2):
                    part_stack[t, zd, p, yy, :, k * LANES : (k + 1) * LANES] = sums[k][
                        half_rows * p : half_rows * (p + 1)
                    ]
            return carry

        lax.fori_loop(0, 2 * Y, one, 0)

    def ya_copy(n, zd):
        return pltpu.make_async_remote_copy(
            src_ref=part_stack.at[0, zd, :, 1 - y],
            dst_ref=recv_ya.at[n],
            send_sem=ya_s.at[n],
            recv_sem=ya_r.at[n],
            device_id=y_peer,
            device_id_type=MESH,
        )

    def yb_copy():
        return pltpu.make_async_remote_copy(
            src_ref=part_stack.at[1, z, :, 1 - y],
            dst_ref=recv_yb,
            send_sem=yb_s,
            recv_sem=yb_r,
            device_id=y_peer,
            device_id_type=MESH,
        )

    def target(way, k):
        return lax.rem(z + k, Z) if way == 0 else lax.rem(z + Z - k, Z)

    def ring_copy(half, way, k, p):
        if half == 0:
            src = part_stack.at[0, target(way, k), p, y]
            dst = recv_a.at[way, k - 1, p]
        else:
            src = part_stack.at[1, target(way, k), p]
            dst = recv_b.at[way, k - 1, p]
        return pltpu.make_async_remote_copy(
            src_ref=src,
            dst_ref=dst,
            send_sem=ring_s.at[half, way, k - 1, p],
            recv_sem=ring_r.at[half, way, k - 1, p],
            device_id=z_peer[way],
            device_id_type=MESH,
        )

    last = H if Z % 2 == 0 else (Z - 1) // 2

    def sent(way, k):
        return [way] if Z % 2 == 0 and k == last else [0, 1]

    sends = []

    def send(copy):
        copy.start()
        sends.append(copy)

    def start_fresh(half, k):
        for way in range(2):
            for p in sent(way, k):
                if k == last or (k == last - 1 and p not in sent(way, last)):
                    send(ring_copy(half, way, k, p))

    def pass_on(half):
        for k in range(last - 1, 0, -1):
            for way in range(2):
                for p in sent(way, k + 1):
                    ring_copy(half, way, k + 1, p).wait_recv()
                    if half == 0:
                        zd = target(way, k)
                        part_stack[0, zd, p, y] = part_stack[0, zd, p, y] + recv_a[way, k, p]
                    else:
                        zd = target(way, k)
                        part_stack[1, zd, p] = part_stack[1, zd, p] + recv_b[way, k, p]
                    send(ring_copy(half, way, k, p))

    groups = [(0, 0)]
    for k in range(1, last + 1):
        ways = [0] if Z % 2 == 0 and k == last else [0, 1]
        groups = [(way, k) for way in ways] + groups

    for n, (way, k) in enumerate(groups):
        zd = target(way, k)
        stack_group(zd)
        if Y > 1:
            send(ya_copy(n, zd))
        if k and (k == last or way == 1):
            start_fresh(1, k)

    pass_on(1)
    for n, (way, k) in enumerate(groups):
        zd = target(way, k)
        if Y > 1:
            ya_copy(n, zd).wait_recv()
            part_stack[0, zd, :, y] = part_stack[0, zd, :, y] + recv_ya[n]
        if k and (k == last or way == 1):
            start_fresh(0, k)
    for p in range(2):
        total = part_stack[1, z, p]
        for way in range(2):
            if last and p in sent(way, 1):
                ring_copy(1, way, 1, p).wait_recv()
                total = total + recv_b[way, 0, p]
        part_stack[1, z, p] = total
    if Y > 1:
        send(yb_copy())
    pass_on(0)
    for p in range(2):
        total = part_stack[0, z, p, y]
        for way in range(2):
            if last and p in sent(way, 1):
                ring_copy(0, way, 1, p).wait_recv()
                total = total + recv_a[way, 0, p]
        start = SUB + half_rows * p
        stack[start : start + half_rows, 0:W] = total
    if Y > 1:
        yb_copy().wait_recv()
    for p in range(2):
        start = SUB + R + half_rows * p
        total = part_stack[1, z, p, y]
        if Y > 1:
            total = total + recv_yb[p]
        stack[start : start + half_rows, 0:W] = total

    tap = tk.shape[1]
    weights = [[power(tk[0, a, b]) for b in range(tap)] for a in range(tap)]
    for i in range(2 * R // SUB):
        def load(a):
            start = SUB * (i + 1) + a - tap // 2
            return stack[start : start + SUB, :]

        trail[SUB * i : SUB * (i + 1), :] = filter_rows(load, weights, tap, wide)[:, :W]

    end = pltpu.make_async_remote_copy(
        src_ref=trail.at[pl.ds(pl.multiple_of(R * (1 - c), SUB), R)],
        dst_ref=trail_in,
        send_sem=end_s,
        recv_sem=end_r,
        device_id=sky,
        device_id_type=MESH,
    )
    send(end)
    end.wait_recv()
    mine = trail[pl.ds(pl.multiple_of(R * c, SUB), R), :]
    theirs = trail_in[...]
    psi = jnp.where(c == 0, mine, theirs)
    phi = jnp.where(c == 0, theirs, mine)
    out[0] = psi / jnp.sqrt(phi + 1.0)

    for e in range(E):
        sky_copy(e).wait_send()
    for copy in sends:
        copy.wait_send()


def shards(expo, science, inv_variance, pixel_masks, point_spread, tile_offset, column_shift, trail_kernel):
    E, R, W = science.shape
    Y = 2 if expo % 2 == 0 else 1
    Z = expo // Y
    K = max(Z // 2, 1)
    half = R // 2
    wide = W + LANES
    f32 = jnp.float32
    dma = pltpu.SemaphoreType.DMA
    hbm = pl.BlockSpec(memory_space=pl.ANY)
    smem = pl.BlockSpec(memory_space=pltpu.SMEM)
    return pl.pallas_call(
        functools.partial(kernel, (E, R, W, Y, Z)),
        out_shape=jax.ShapeDtypeStruct((1, R, W), f32),
        in_specs=[hbm] * 3 + [smem] * 4,
        out_specs=pl.BlockSpec(memory_space=pltpu.VMEM),
        scratch_shapes=[
            pltpu.VMEM((E, R, W), f32),
            pltpu.VMEM((E, R, W), f32),
            pltpu.VMEM((E, R, W), jnp.int32),
            pltpu.VMEM((E, 2 * R + 2 * SUB, wide), f32),
            pltpu.VMEM((E, R, W), f32),
            pltpu.VMEM((E, 2, W // LANES + 3, R, LANES), f32),
            pltpu.VMEM((2, Z, 2, Y, half, W), f32),
            pltpu.VMEM((Z, 2, half, W), f32),
            pltpu.VMEM((2, half, W), f32),
            pltpu.VMEM((2, K, 2, half, W), f32),
            pltpu.VMEM((2, K, 2, Y, half, W), f32),
            pltpu.VMEM((2 * R + 2 * SUB, wide), f32),
            pltpu.VMEM((2 * R, W), f32),
            pltpu.VMEM((R, W), f32),
            dma((3, E)),
            dma((E,)),
            dma((E,)),
            dma((Z,)),
            dma((Z,)),
            dma,
            dma,
            dma((2, 2, K, 2)),
            dma((2, 2, K, 2)),
            dma,
            dma,
        ],
        compiler_params=pltpu.CompilerParams(collective_id=0, has_side_effects=True),
    )(science, inv_variance, pixel_masks, point_spread, tile_offset, column_shift, trail_kernel)


def solution(mesh):
    return jax.shard_map(
        functools.partial(shards, mesh.shape["expo"]),
        mesh=mesh,
        in_specs=(
            P(("field", "expo"), "sky", None),
            P(("field", "expo"), "sky", None),
            P(("field", "expo"), "sky", None),
            P(("field", "expo"), None, None),
            P(None, "expo"),
            P(None, "expo"),
            P("expo", None, None),
        ),
        out_specs=P(("field", "expo"), "sky", None),
        check_vma=False,
    )
```

```python
import functools

import jax
import jax.numpy as jnp
from jax import lax
from jax.experimental import pallas as pl
from jax.experimental.pallas import tpu as pltpu
from jax.sharding import PartitionSpec as P

LANES = 128
SUB = 8
FIRST = 3
MESH = pl.DeviceIdType.MESH


def filter_rows(load, weights, taps, wide):
    sums = [None] * taps
    for a in range(taps):
        x = load(a)
        for b in range(taps):
            term = weights[a][b] * x
            sums[b] = term if sums[b] is None else sums[b] + term
    mid = taps // 2
    total = sums[mid]
    for b in range(taps):
        if b != mid:
            total = total + pltpu.roll(sums[b], (mid - b) % wide, 1)
    return total


def kernel(
    dims,
    sci, iv, msk, ps, off, shf, tk, out,
    sci_v, iv_v, msk_v, image, other, filt, part_stack,
    recv_ya, recv_yb, recv_a, recv_b, stack, trail, trail_in,
    in_sem, sky_s, sky_r, ya_s, ya_r, yb_s, yb_r, line_s, line_r, end_s, end_r,
):
    E, R, W, Y, Z = dims
    taps = ps.shape[0]
    wide = W + LANES
    band = R // 2
    tiles = W // LANES
    c = lax.axis_index("sky")
    me = lax.axis_index("expo")
    y = lax.rem(me, Y)
    z = me // Y
    sky = {"sky": 1 - c}
    y_peer = {"expo": z * Y + (Y - 1 - y)}
    loads = []
    for e in range(E):
        trio = [
            pltpu.make_async_copy(src.at[e], dst.at[e], in_sem.at[n, e])
            for n, (src, dst) in enumerate(((iv, iv_v), (msk, msk_v), (sci, sci_v)))
        ]
        for copy in trio:
            copy.start()
        loads.append(trio)

    barrier = pltpu.get_barrier_semaphore()
    for peer in [sky] + ([y_peer] if Y > 1 else []):
        pl.semaphore_signal(barrier, inc=1, device_id=peer, device_id_type=MESH)

    @pl.when(z > 0)
    def _():
        pl.semaphore_signal(barrier, inc=1, device_id={"expo": me - Y}, device_id_type=MESH)

    @pl.when(z < Z - 1)
    def _():
        pl.semaphore_signal(barrier, inc=1, device_id={"expo": me + Y}, device_id_type=MESH)

    greeted = (2 if Y > 1 else 1) + jnp.where(z > 0, 1, 0) + jnp.where(z < Z - 1, 1, 0)

    top = 2 * R + SUB
    for e in range(E):
        image[e, 0:SUB, :] = jnp.zeros((SUB, wide), jnp.float32)
        image[e, top : top + SUB, :] = jnp.zeros((SUB, wide), jnp.float32)
        image[e, SUB:top, W:wide] = jnp.zeros((2 * R, LANES), jnp.float32)
        for t in range(2):
            for m in (0, tiles + 1, tiles + 2):
                filt[e, t, m] = jnp.zeros((R, LANES), jnp.float32)
    stack[0:SUB, :] = jnp.zeros((SUB, wide), jnp.float32)
    stack[top : top + SUB, :] = jnp.zeros((SUB, wide), jnp.float32)
    stack[SUB:top, W:wide] = jnp.zeros((2 * R, LANES), jnp.float32)

    own_rows = pl.ds(pl.multiple_of(SUB + R * c, SUB), R)

    def sky_copy(e):
        return pltpu.make_async_remote_copy(
            src_ref=other.at[e],
            dst_ref=image.at[e, own_rows, pl.ds(0, W)],
            send_sem=sky_s.at[e],
            recv_sem=sky_r.at[e],
            device_id=sky,
            device_id_type=MESH,
        )

    for e in range(E):
        for copy in loads[e]:
            copy.wait()
        w = iv_v[e] * msk_v[e].astype(jnp.float32)
        s = sci_v[e] * w
        image[e, own_rows, 0:W] = jnp.where(c == 0, s, w)
        other[e] = jnp.where(c == 0, w, s)
        if e == 0:
            pl.semaphore_wait(barrier, greeted)
        sky_copy(e).start()

    def power(value):
        return jnp.where(c == 0, value, value * value)

    def filter_one(e, carry):
        weights = [[power(ps[a, e, b]) for b in range(taps)] for a in range(taps)]
        sky_copy(e).wait_recv()
        for i in range(2 * R // SUB):
            def load(a):
                start = SUB * (i + 1) + a - taps // 2
                return image[e, start : start + SUB, :]

            total = filter_rows(load, weights, taps, wide)
            t, low = divmod(SUB * i, R)
            for k in range(tiles):
                filt[e, t, k + 1, low : low + SUB, :] = total[:, k * LANES : (k + 1) * LANES]
        return carry

    lax.fori_loop(0, E, filter_one, 0)

    lane = lax.broadcasted_iota(jnp.int32, (R, LANES), 1)

    def stack_group(zd):
        def one(yy, carry):
            v = zd * Y + yy
            sums = [[None] * tiles for _ in range(2)]
            for e in range(E):
                o = LANES - shf[e, v]
                q = o // LANES
                r = o - q * LANES
                near = lane < LANES - r
                o_row = off[e, v]
                for t in range(2):
                    source = t + o_row - 2 * t * o_row
                    turned = [pltpu.roll(filt[e, source, q + m], LANES - r, 1) for m in range(tiles + 1)]
                    for k in range(tiles):
                        got = jnp.where(near, turned[k], turned[k + 1])
                        sums[t][k] = got if sums[t][k] is None else sums[t][k] + got
            for t in range(2):
                for k in range(tiles):
                    for p in range(2):
                        rows = sums[t][k][band * p : band * (p + 1)]
                        part_stack[zd, 2 * t + p, yy, :, k * LANES : (k + 1) * LANES] = rows
            return carry

        lax.fori_loop(0, Y, one, 0)

    def ya_copy(n):
        return pltpu.make_async_remote_copy(
            src_ref=part_stack.at[order(n), pl.ds(0, FIRST), 1 - y],
            dst_ref=recv_ya.at[n],
            send_sem=ya_s.at[n],
            recv_sem=ya_r.at[n],
            device_id=y_peer,
            device_id_type=MESH,
        )

    def yb_copy():
        return pltpu.make_async_remote_copy(
            src_ref=part_stack.at[z, FIRST, 1 - y],
            dst_ref=recv_yb,
            send_sem=yb_s,
            recv_sem=yb_r,
            device_id=y_peer,
            device_id_type=MESH,
        )

    def order(n):
        return jnp.where(2 * z < Z, Z - 1 - n, n)

    def line_copy(way, d, g):
        if g < FIRST:
            src = part_stack.at[d, g, y]
            dst = recv_a.at[way, d, g]
        else:
            src = part_stack.at[d, g]
            dst = recv_b.at[way, d]
        return pltpu.make_async_remote_copy(
            src_ref=src,
            dst_ref=dst,
            send_sem=line_s.at[way, d, g],
            recv_sem=line_r.at[way, d, g],
            device_id={"expo": me + Y * (1 - 2 * way)},
            device_id_type=MESH,
        )

    def take(way, d, g):
        line_copy(way, d, g).wait_recv()
        if g < FIRST:
            part_stack[d, g, y] = part_stack[d, g, y] + recv_a[way, d, g]
        else:
            part_stack[d, g] = part_stack[d, g] + recv_b[way, d]

    def pass_on(n, g):
        d = order(n)
        way = jnp.where(d > z, 0, 1)

        @pl.when(d != z)
        def _():
            @pl.when((1 - way) * z + way * (Z - 1 - z) > 0)
            def _():
                take(way, d, g)

            line_copy(way, d, g).start()

    def finish(g):
        @pl.when(z > 0)
        def _():
            take(0, z, g)

        @pl.when(z < Z - 1)
        def _():
            take(1, z, g)

    for n in range(Z):
        stack_group(order(n))
        if Y > 1:
            ya_copy(n).start()

        @pl.when((z == 0) | (z == Z - 1))
        def _():
            pass_on(n, FIRST)

    @pl.when((z > 0) & (z < Z - 1))
    def _():
        for n in range(Z):
            pass_on(n, FIRST)

    for n in range(Z):
        if Y > 1:
            d = order(n)
            ya_copy(n).wait_recv()
            part_stack[d, 0:FIRST, y] = part_stack[d, 0:FIRST, y] + recv_ya[n]
        for g in range(FIRST):
            pass_on(n, g)
    finish(FIRST)
    if Y > 1:
        yb_copy().start()
    for g in range(FIRST):
        finish(g)
        start = SUB + band * g
        stack[start : start + band, 0:W] = part_stack[z, g, y]
    start = SUB + band * FIRST
    if Y > 1:
        yb_copy().wait_recv()
        stack[start : start + band, 0:W] = part_stack[z, FIRST, y] + recv_yb[...]
    else:
        stack[start : start + band, 0:W] = part_stack[z, FIRST, y]

    tap = tk.shape[0]
    weights = [[power(tk[a, 0, b]) for b in range(tap)] for a in range(tap)]
    for i in range(2 * R // SUB):
        def load(a):
            start = SUB * (i + 1) + a - tap // 2
            return stack[start : start + SUB, :]

        trail[SUB * i : SUB * (i + 1), :] = filter_rows(load, weights, tap, wide)[:, :W]

    end = pltpu.make_async_remote_copy(
        src_ref=trail.at[pl.ds(pl.multiple_of(R * (1 - c), SUB), R)],
        dst_ref=trail_in,
        send_sem=end_s,
        recv_sem=end_r,
        device_id=sky,
        device_id_type=MESH,
    )
    end.start()
    end.wait_recv()
    mine = trail[pl.ds(pl.multiple_of(R * c, SUB), R), :]
    theirs = trail_in[...]
    psi = jnp.where(c == 0, mine, theirs)
    phi = jnp.where(c == 0, theirs, mine)
    out[0] = psi / jnp.sqrt(phi + 1.0)

    for e in range(E):
        sky_copy(e).wait_send()
    end.wait_send()
    if Y > 1:
        yb_copy().wait_send()
        for n in range(Z):
            ya_copy(n).wait_send()
    for n in range(Z):
        d = order(n)

        @pl.when(d != z)
        def _():
            for g in range(FIRST + 1):
                line_copy(jnp.where(d > z, 0, 1), d, g).wait_send()


def shards(expo, science, inv_variance, pixel_masks, point_spread, tile_offset, column_shift, trail_kernel):
    E, R, W = science.shape
    Y = 2 if expo % 2 == 0 else 1
    Z = expo // Y
    band = R // 2
    wide = W + LANES
    f32 = jnp.float32
    dma = pltpu.SemaphoreType.DMA
    hbm = pl.BlockSpec(memory_space=pl.ANY)
    smem = pl.BlockSpec(memory_space=pltpu.SMEM)
    return pl.pallas_call(
        functools.partial(kernel, (E, R, W, Y, Z)),
        out_shape=jax.ShapeDtypeStruct((1, R, W), f32),
        in_specs=[hbm] * 3 + [smem] * 4,
        out_specs=pl.BlockSpec(memory_space=pltpu.VMEM),
        scratch_shapes=[
            pltpu.VMEM((E, R, W), f32),
            pltpu.VMEM((E, R, W), f32),
            pltpu.VMEM((E, R, W), jnp.int32),
            pltpu.VMEM((E, 2 * R + 2 * SUB, wide), f32),
            pltpu.VMEM((E, R, W), f32),
            pltpu.VMEM((E, 2, W // LANES + 3, R, LANES), f32),
            pltpu.VMEM((Z, FIRST + 1, Y, band, W), f32),
            pltpu.VMEM((Z, FIRST, band, W), f32),
            pltpu.VMEM((band, W), f32),
            pltpu.VMEM((2, Z, FIRST, band, W), f32),
            pltpu.VMEM((2, Z, Y, band, W), f32),
            pltpu.VMEM((2 * R + 2 * SUB, wide), f32),
            pltpu.VMEM((2 * R, W), f32),
            pltpu.VMEM((R, W), f32),
            dma((3, E)),
            dma((E,)),
            dma((E,)),
            dma((Z,)),
            dma((Z,)),
            dma,
            dma,
            dma((2, Z, FIRST + 1)),
            dma((2, Z, FIRST + 1)),
            dma,
            dma,
        ],
        compiler_params=pltpu.CompilerParams(collective_id=0, has_side_effects=True),
    )(
        science,
        inv_variance,
        pixel_masks,
        jnp.transpose(point_spread, (1, 0, 2)),
        tile_offset.T,
        column_shift.T,
        jnp.transpose(trail_kernel, (1, 0, 2)),
    )


def solution(mesh):
    return jax.shard_map(
        functools.partial(shards, mesh.shape["expo"]),
        mesh=mesh,
        in_specs=(
            P(("field", "expo"), "sky", None),
            P(("field", "expo"), "sky", None),
            P(("field", "expo"), "sky", None),
            P(("field", "expo"), None, None),
            P(None, "expo"),
            P(None, "expo"),
            P("expo", None, None),
        ),
        out_specs=P(("field", "expo"), "sky", None),
        check_vma=False,
    )
```

```python
import functools

import jax
import jax.numpy as jnp
from jax import lax
from jax.experimental import pallas as pl
from jax.experimental.pallas import tpu as pltpu
from jax.sharding import PartitionSpec as P

LANES = 128
SUB = 8
FIRST = 3
MESH = pl.DeviceIdType.MESH


def filter_rows(load, weights, taps):
    sums = [None] * taps
    for a in range(taps):
        x = load(a)
        for b in range(taps):
            term = weights[a][b] * x
            sums[b] = term if sums[b] is None else sums[b] + term
    mid = taps // 2
    width = sums[0].shape[1]
    tiles = width // LANES
    lane = lax.broadcasted_iota(jnp.int32, (sums[0].shape[0], LANES), 1)
    total = [sums[mid][:, LANES * k : LANES * (k + 1)] for k in range(tiles)]
    for b in range(taps):
        if b == mid:
            continue
        turned = pltpu.roll(sums[b], (mid - b) % width, 1)
        for k in range(tiles):
            piece = turned[:, LANES * k : LANES * (k + 1)]
            if b < mid and k == 0:
                piece = jnp.where(lane >= mid - b, piece, 0.0)
            if b > mid and k == tiles - 1:
                piece = jnp.where(lane < LANES - (b - mid), piece, 0.0)
            total[k] = total[k] + piece
    return total


def kernel(
    dims,
    sci, iv, msk, ps_in, off_in, shf_in, tk_in, out,
    ps, off, shf, tk,
    sci_v, iv_v, msk_v, image, other, filt, part_stack,
    recv_ya, recv_yb, recv_a, recv_b, stack, trail, trail_in,
    in_sem, small_sem, sky_s, sky_r, ya_s, ya_r, yb_s, yb_r, line_s, line_r, end_s, end_r,
):
    E, R, W, Y, Z = dims
    taps = ps.shape[0]
    band = R // 2
    tiles = W // LANES
    c = lax.axis_index("sky")
    me = lax.axis_index("expo")
    y = lax.rem(me, Y)
    z = me // Y
    sky = {"sky": 1 - c}
    y_peer = {"expo": z * Y + (Y - 1 - y)}
    barrier = pltpu.get_barrier_semaphore()
    for peer in [sky] + ([y_peer] if Y > 1 else []):
        pl.semaphore_signal(barrier, inc=1, device_id=peer, device_id_type=MESH)

    @pl.when(z > 0)
    def _():
        pl.semaphore_signal(barrier, inc=1, device_id={"expo": me - Y}, device_id_type=MESH)

    @pl.when(z < Z - 1)
    def _():
        pl.semaphore_signal(barrier, inc=1, device_id={"expo": me + Y}, device_id_type=MESH)

    greeted = (2 if Y > 1 else 1) + jnp.where(z > 0, 1, 0) + jnp.where(z < Z - 1, 1, 0)

    loads = []
    for e in range(E):
        trio = [
            pltpu.make_async_copy(src.at[e], dst.at[e], in_sem.at[n, e])
            for n, (src, dst) in enumerate(((iv, iv_v), (msk, msk_v), (sci, sci_v)))
        ]
        for copy in trio:
            copy.start()
        loads.append(trio)

    small = [
        pltpu.make_async_copy(src, dst, small_sem.at[n])
        for n, (src, dst) in enumerate(((ps_in, ps), (off_in, off), (shf_in, shf), (tk_in, tk)))
    ]
    for copy in small:
        copy.start()

    top = 2 * R + SUB
    for e in range(E):
        image[e, 0:SUB, :] = jnp.zeros((SUB, W), jnp.float32)
        image[e, top : top + SUB, :] = jnp.zeros((SUB, W), jnp.float32)
        for t in range(2):
            for m in (0, tiles + 1, tiles + 2):
                filt[e, t, m] = jnp.zeros((R, LANES), jnp.float32)
    stack[0:SUB, :] = jnp.zeros((SUB, W), jnp.float32)
    stack[top : top + SUB, :] = jnp.zeros((SUB, W), jnp.float32)

    own_rows = pl.ds(pl.multiple_of(SUB + R * c, SUB), R)

    def sky_copy(e):
        return pltpu.make_async_remote_copy(
            src_ref=other.at[e],
            dst_ref=image.at[e, own_rows, pl.ds(0, W)],
            send_sem=sky_s.at[e],
            recv_sem=sky_r.at[e],
            device_id=sky,
            device_id_type=MESH,
        )

    for e in range(E):
        for copy in loads[e]:
            copy.wait()
        w = iv_v[e] * msk_v[e].astype(jnp.float32)
        s = sci_v[e] * w
        image[e, own_rows, 0:W] = jnp.where(c == 0, s, w)
        other[e] = jnp.where(c == 0, w, s)

    def power(value):
        return jnp.where(c == 0, value, value * value)

    def filter_chunks(e, chunks):
        weights = [[power(ps[a, e, b]) for b in range(taps)] for a in range(taps)]
        for i in chunks:
            def load(a):
                start = SUB * (i + 1) + a - taps // 2
                return image[e, start : start + SUB, :]

            t, low = divmod(SUB * i, R)
            for k, piece in enumerate(filter_rows(load, weights, taps)):
                filt[e, t, k + 1, low : low + SUB, :] = piece

    for copy in small:
        copy.wait()
    chunks = R // SUB
    own_chunks = (range(0, chunks - 1), range(chunks + 1, 2 * chunks))
    late_chunks = (range(chunks - 1, 2 * chunks), range(0, chunks + 1))

    def own_filter(e, carry):
        for side in range(2):
            @pl.when(c == side)
            def _():
                filter_chunks(e, own_chunks[side])
        return carry

    def late_filter(e, carry):
        sky_copy(e).wait_recv()
        for side in range(2):
            @pl.when(c == side)
            def _():
                filter_chunks(e, late_chunks[side])
        return carry

    lax.fori_loop(0, E, own_filter, 0)
    pl.semaphore_wait(barrier, greeted)
    for e in range(E):
        sky_copy(e).start()
    lax.fori_loop(0, E, late_filter, 0)

    lane = lax.broadcasted_iota(jnp.int32, (R, LANES), 1)

    def stack_group(zd):
        def one(yy, carry):
            v = zd * Y + yy
            sums = [[None] * tiles for _ in range(2)]
            for e in range(E):
                o = LANES - shf[e, v]
                q = o // LANES
                r = o - q * LANES
                near = lane < LANES - r
                o_row = off[e, v]
                for t in range(2):
                    source = t + o_row - 2 * t * o_row
                    turned = [pltpu.roll(filt[e, source, q + m], LANES - r, 1) for m in range(tiles + 1)]
                    for k in range(tiles):
                        got = jnp.where(near, turned[k], turned[k + 1])
                        sums[t][k] = got if sums[t][k] is None else sums[t][k] + got
            for t in range(2):
                for k in range(tiles):
                    for p in range(2):
                        rows = sums[t][k][band * p : band * (p + 1)]
                        part_stack[zd, 2 * t + p, yy, :, k * LANES : (k + 1) * LANES] = rows
            return carry

        lax.fori_loop(0, Y, one, 0)

    def ya_copy(n):
        return pltpu.make_async_remote_copy(
            src_ref=part_stack.at[order(n), pl.ds(0, FIRST), 1 - y],
            dst_ref=recv_ya.at[n],
            send_sem=ya_s.at[n],
            recv_sem=ya_r.at[n],
            device_id=y_peer,
            device_id_type=MESH,
        )

    def yb_copy():
        return pltpu.make_async_remote_copy(
            src_ref=part_stack.at[z, FIRST, 1 - y],
            dst_ref=recv_yb,
            send_sem=yb_s,
            recv_sem=yb_r,
            device_id=y_peer,
            device_id_type=MESH,
        )

    def order(n):
        return jnp.where(2 * z < Z, Z - 1 - n, n)

    def line_copy(way, d, g):
        if g < FIRST:
            src = part_stack.at[d, g, y]
            dst = recv_a.at[way, d, g]
        else:
            src = part_stack.at[d, g]
            dst = recv_b.at[way, d]
        return pltpu.make_async_remote_copy(
            src_ref=src,
            dst_ref=dst,
            send_sem=line_s.at[way, d, g],
            recv_sem=line_r.at[way, d, g],
            device_id={"expo": me + Y * (1 - 2 * way)},
            device_id_type=MESH,
        )

    def take(way, d, g):
        line_copy(way, d, g).wait_recv()
        if g < FIRST:
            part_stack[d, g, y] = part_stack[d, g, y] + recv_a[way, d, g]
        else:
            part_stack[d, g] = part_stack[d, g] + recv_b[way, d]

    def pass_on(n, g):
        d = order(n)
        way = jnp.where(d > z, 0, 1)

        @pl.when(d != z)
        def _():
            @pl.when((1 - way) * z + way * (Z - 1 - z) > 0)
            def _():
                take(way, d, g)

            line_copy(way, d, g).start()

    def finish(g):
        @pl.when(z > 0)
        def _():
            take(0, z, g)

        @pl.when(z < Z - 1)
        def _():
            take(1, z, g)

    for n in range(Z):
        stack_group(order(n))
        if Y > 1:
            ya_copy(n).start()

        @pl.when((z == 0) | (z == Z - 1))
        def _():
            pass_on(n, FIRST)

    @pl.when((z > 0) & (z < Z - 1))
    def _():
        for n in range(Z):
            pass_on(n, FIRST)

    for n in range(Z):
        if Y > 1:
            d = order(n)
            ya_copy(n).wait_recv()
            part_stack[d, 0:FIRST, y] = part_stack[d, 0:FIRST, y] + recv_ya[n]
        for g in range(FIRST):
            pass_on(n, g)
    finish(FIRST)
    if Y > 1:
        yb_copy().start()
    for g in range(FIRST):
        finish(g)
        start = SUB + band * g
        stack[start : start + band, 0:W] = part_stack[z, g, y]
    start = SUB + band * FIRST
    if Y > 1:
        yb_copy().wait_recv()
        stack[start : start + band, 0:W] = part_stack[z, FIRST, y] + recv_yb[...]
    else:
        stack[start : start + band, 0:W] = part_stack[z, FIRST, y]

    tap = tk.shape[0]
    weights = [[power(tk[a, 0, b]) for b in range(tap)] for a in range(tap)]
    for i in range(2 * R // SUB):
        def load(a):
            start = SUB * (i + 1) + a - tap // 2
            return stack[start : start + SUB, :]

        for k, piece in enumerate(filter_rows(load, weights, tap)):
            trail[SUB * i : SUB * (i + 1), LANES * k : LANES * (k + 1)] = piece

    end = pltpu.make_async_remote_copy(
        src_ref=trail.at[pl.ds(pl.multiple_of(R * (1 - c), SUB), R)],
        dst_ref=trail_in,
        send_sem=end_s,
        recv_sem=end_r,
        device_id=sky,
        device_id_type=MESH,
    )
    end.start()
    end.wait_recv()
    mine = trail[pl.ds(pl.multiple_of(R * c, SUB), R), :]
    theirs = trail_in[...]
    psi = jnp.where(c == 0, mine, theirs)
    phi = jnp.where(c == 0, theirs, mine)
    out[0] = psi / jnp.sqrt(phi + 1.0)

    for e in range(E):
        sky_copy(e).wait_send()
    end.wait_send()
    if Y > 1:
        yb_copy().wait_send()
        for n in range(Z):
            ya_copy(n).wait_send()
    for n in range(Z):
        d = order(n)

        @pl.when(d != z)
        def _():
            for g in range(FIRST + 1):
                line_copy(jnp.where(d > z, 0, 1), d, g).wait_send()


def shards(expo, science, inv_variance, pixel_masks, point_spread, tile_offset, column_shift, trail_kernel):
    E, R, W = science.shape
    Y = 2 if expo % 2 == 0 else 1
    Z = expo // Y
    band = R // 2
    taps = point_spread.shape[1]
    f32 = jnp.float32
    dma = pltpu.SemaphoreType.DMA
    hbm = pl.BlockSpec(memory_space=pl.ANY)
    return pl.pallas_call(
        functools.partial(kernel, (E, R, W, Y, Z)),
        out_shape=jax.ShapeDtypeStruct((1, R, W), f32),
        in_specs=[hbm] * 7,
        out_specs=pl.BlockSpec(memory_space=pltpu.VMEM),
        scratch_shapes=[
            pltpu.SMEM((taps, E, taps), f32),
            pltpu.SMEM(tile_offset.shape[::-1], jnp.int32),
            pltpu.SMEM(column_shift.shape[::-1], jnp.int32),
            pltpu.SMEM((trail_kernel.shape[1], 1, trail_kernel.shape[2]), f32),
            pltpu.VMEM((E, R, W), f32),
            pltpu.VMEM((E, R, W), f32),
            pltpu.VMEM((E, R, W), jnp.int32),
            pltpu.VMEM((E, 2 * R + 2 * SUB, W), f32),
            pltpu.VMEM((E, R, W), f32),
            pltpu.VMEM((E, 2, W // LANES + 3, R, LANES), f32),
            pltpu.VMEM((Z, FIRST + 1, Y, band, W), f32),
            pltpu.VMEM((Z, FIRST, band, W), f32),
            pltpu.VMEM((band, W), f32),
            pltpu.VMEM((2, Z, FIRST, band, W), f32),
            pltpu.VMEM((2, Z, Y, band, W), f32),
            pltpu.VMEM((2 * R + 2 * SUB, W), f32),
            pltpu.VMEM((2 * R, W), f32),
            pltpu.VMEM((R, W), f32),
            dma((3, E)),
            dma((4,)),
            dma((E,)),
            dma((E,)),
            dma((Z,)),
            dma((Z,)),
            dma,
            dma,
            dma((2, Z, FIRST + 1)),
            dma((2, Z, FIRST + 1)),
            dma,
            dma,
        ],
        compiler_params=pltpu.CompilerParams(collective_id=0, has_side_effects=True),
    )(
        science,
        inv_variance,
        pixel_masks,
        jnp.transpose(point_spread, (1, 0, 2)),
        tile_offset.T,
        column_shift.T,
        jnp.transpose(trail_kernel, (1, 0, 2)),
    )


def solution(mesh):
    return jax.shard_map(
        functools.partial(shards, mesh.shape["expo"]),
        mesh=mesh,
        in_specs=(
            P(("field", "expo"), "sky", None),
            P(("field", "expo"), "sky", None),
            P(("field", "expo"), "sky", None),
            P(("field", "expo"), None, None),
            P(None, "expo"),
            P(None, "expo"),
            P("expo", None, None),
        ),
        out_specs=P(("field", "expo"), "sky", None),
        check_vma=False,
    )
```

```python
import functools

import jax
import jax.numpy as jnp
from jax import lax
from jax.experimental import pallas as pl
from jax.experimental.pallas import tpu as pltpu
from jax.sharding import PartitionSpec as P

LANES = 128
SUB = 8
FIRST = 3
MESH = pl.DeviceIdType.MESH


def filter_rows(load, weights, taps):
    sums = [None] * taps
    for a in range(taps):
        x = load(a)
        for b in range(taps):
            term = weights[a][b] * x
            sums[b] = term if sums[b] is None else sums[b] + term
    mid = taps // 2
    width = sums[0].shape[1]
    tiles = width // LANES
    lane = lax.broadcasted_iota(jnp.int32, (sums[0].shape[0], LANES), 1)
    total = [sums[mid][:, LANES * k : LANES * (k + 1)] for k in range(tiles)]
    for b in range(taps):
        if b == mid:
            continue
        turned = pltpu.roll(sums[b], (mid - b) % width, 1)
        for k in range(tiles):
            piece = turned[:, LANES * k : LANES * (k + 1)]
            if b < mid and k == 0:
                piece = jnp.where(lane >= mid - b, piece, 0.0)
            if b > mid and k == tiles - 1:
                piece = jnp.where(lane < LANES - (b - mid), piece, 0.0)
            total[k] = total[k] + piece
    return total


def kernel(
    dims,
    sci, iv, msk, ps_in, off_in, shf_in, tk_in, out,
    ps, off, shf, tk,
    sci_v, iv_v, msk_v, image, other, filt, part_stack,
    recv_ya, recv_yb, recv_a, recv_b, stack, trail, trail_in,
    in_sem, small_sem, sky_s, sky_r, ya_s, ya_r, yb_s, yb_r, line_s, line_r, end_s, end_r,
):
    E, R, W, Y, Z = dims
    taps = ps.shape[0]
    band = R // 2
    tiles = W // LANES
    c = lax.axis_index("sky")
    me = lax.axis_index("expo")
    y = lax.rem(me, Y)
    z = me // Y
    sky = {"sky": 1 - c}
    y_peer = {"expo": z * Y + (Y - 1 - y)}
    barrier = pltpu.get_barrier_semaphore()
    for peer in [sky] + ([y_peer] if Y > 1 else []):
        pl.semaphore_signal(barrier, inc=1, device_id=peer, device_id_type=MESH)

    @pl.when(z > 0)
    def _():
        pl.semaphore_signal(barrier, inc=1, device_id={"expo": me - Y}, device_id_type=MESH)

    @pl.when(z < Z - 1)
    def _():
        pl.semaphore_signal(barrier, inc=1, device_id={"expo": me + Y}, device_id_type=MESH)

    greeted = (2 if Y > 1 else 1) + jnp.where(z > 0, 1, 0) + jnp.where(z < Z - 1, 1, 0)

    loads = []
    for e in range(E):
        trio = [
            pltpu.make_async_copy(src.at[e], dst.at[e], in_sem.at[n, e])
            for n, (src, dst) in enumerate(((iv, iv_v), (msk, msk_v), (sci, sci_v)))
        ]
        for copy in trio:
            copy.start()
        loads.append(trio)

    small = [
        pltpu.make_async_copy(src, dst, small_sem.at[n])
        for n, (src, dst) in enumerate(((ps_in, ps), (off_in, off), (shf_in, shf), (tk_in, tk)))
    ]
    for copy in small:
        copy.start()

    top = 2 * R + SUB
    for e in range(E):
        image[e, 0:SUB, :] = jnp.zeros((SUB, W), jnp.float32)
        image[e, top : top + SUB, :] = jnp.zeros((SUB, W), jnp.float32)
        for t in range(2):
            for m in (0, tiles + 1, tiles + 2):
                filt[e, t, m] = jnp.zeros((R, LANES), jnp.float32)
    stack[0:SUB, :] = jnp.zeros((SUB, W), jnp.float32)
    stack[top : top + SUB, :] = jnp.zeros((SUB, W), jnp.float32)

    own_rows = pl.ds(pl.multiple_of(SUB + R * c, SUB), R)

    def sky_copy(e):
        return pltpu.make_async_remote_copy(
            src_ref=other.at[e],
            dst_ref=image.at[e, own_rows, pl.ds(0, W)],
            send_sem=sky_s.at[e],
            recv_sem=sky_r.at[e],
            device_id=sky,
            device_id_type=MESH,
        )

    for e in range(E):
        for copy in loads[e]:
            copy.wait()
        w = iv_v[e] * msk_v[e].astype(jnp.float32)
        s = sci_v[e] * w
        image[e, own_rows, 0:W] = jnp.where(c == 0, s, w)
        other[e] = jnp.where(c == 0, w, s)

    def power(value):
        return jnp.where(c == 0, value, value * value)

    def filter_chunks(e, chunks):
        weights = [[power(ps[a, e, b]) for b in range(taps)] for a in range(taps)]
        for i in chunks:
            def load(a):
                start = SUB * (i + 1) + a - taps // 2
                return image[e, start : start + SUB, :]

            t, low = divmod(SUB * i, R)
            for k, piece in enumerate(filter_rows(load, weights, taps)):
                filt[e, t, k + 1, low : low + SUB, :] = piece

    for copy in small:
        copy.wait()
    chunks = R // SUB
    own_chunks = (range(0, chunks - 1), range(chunks + 1, 2 * chunks))
    late_chunks = (range(chunks - 1, 2 * chunks), range(0, chunks + 1))

    def own_filter(e, carry):
        for side in range(2):
            @pl.when(c == side)
            def _():
                filter_chunks(e, own_chunks[side])
        return carry

    def late_filter(e, carry):
        sky_copy(e).wait_recv()
        for side in range(2):
            @pl.when(c == side)
            def _():
                filter_chunks(e, late_chunks[side])
        return carry

    lax.fori_loop(0, E, own_filter, 0)
    pl.semaphore_wait(barrier, greeted)
    for e in range(E):
        sky_copy(e).start()
    lax.fori_loop(0, E, late_filter, 0)

    lane = lax.broadcasted_iota(jnp.int32, (R, LANES), 1)

    def stack_group(zd):
        def one(yy, carry):
            v = zd * Y + yy
            sums = [[None] * tiles for _ in range(2)]
            for e in range(E):
                o = LANES - shf[e, v]
                q = o // LANES
                r = o - q * LANES
                near = lane < LANES - r
                o_row = off[e, v]
                for t in range(2):
                    source = t + o_row - 2 * t * o_row
                    turned = [pltpu.roll(filt[e, source, q + m], LANES - r, 1) for m in range(tiles + 1)]
                    for k in range(tiles):
                        got = jnp.where(near, turned[k], turned[k + 1])
                        sums[t][k] = got if sums[t][k] is None else sums[t][k] + got
            for t in range(2):
                for k in range(tiles):
                    for p in range(2):
                        rows = sums[t][k][band * p : band * (p + 1)]
                        part_stack[zd, 2 * t + p, yy, :, k * LANES : (k + 1) * LANES] = rows
            return carry

        lax.fori_loop(0, Y, one, 0)

    def ya_copy(n):
        return pltpu.make_async_remote_copy(
            src_ref=part_stack.at[order(n), pl.ds(0, FIRST), 1 - y],
            dst_ref=recv_ya.at[n],
            send_sem=ya_s.at[n],
            recv_sem=ya_r.at[n],
            device_id=y_peer,
            device_id_type=MESH,
        )

    def yb_copy():
        return pltpu.make_async_remote_copy(
            src_ref=part_stack.at[z, FIRST, 1 - y],
            dst_ref=recv_yb,
            send_sem=yb_s,
            recv_sem=yb_r,
            device_id=y_peer,
            device_id_type=MESH,
        )

    def order(n):
        return jnp.where(2 * z < Z, Z - 1 - n, n)

    def line_copy(way, d, g):
        if g < FIRST:
            src = part_stack.at[d, g, y]
            dst = recv_a.at[way, d, g]
        else:
            src = part_stack.at[d, g]
            dst = recv_b.at[way, d]
        return pltpu.make_async_remote_copy(
            src_ref=src,
            dst_ref=dst,
            send_sem=line_s.at[way, d, g],
            recv_sem=line_r.at[way, d, g],
            device_id={"expo": me + Y * (1 - 2 * way)},
            device_id_type=MESH,
        )

    def take(way, d, g):
        line_copy(way, d, g).wait_recv()
        if g < FIRST:
            part_stack[d, g, y] = part_stack[d, g, y] + recv_a[way, d, g]
        else:
            part_stack[d, g] = part_stack[d, g] + recv_b[way, d]

    def pass_on(n, g):
        d = order(n)
        way = jnp.where(d > z, 0, 1)

        @pl.when(d != z)
        def _():
            @pl.when((1 - way) * z + way * (Z - 1 - z) > 0)
            def _():
                take(way, d, g)

            line_copy(way, d, g).start()

    def finish(g):
        @pl.when(z > 0)
        def _():
            take(0, z, g)

        @pl.when(z < Z - 1)
        def _():
            take(1, z, g)

    for n in range(Z):
        stack_group(order(n))
        if Y > 1:
            ya_copy(n).start()

        @pl.when((z == 0) | (z == Z - 1))
        def _():
            pass_on(n, FIRST)

    @pl.when((z > 0) & (z < Z - 1))
    def _():
        for n in range(Z):
            pass_on(n, FIRST)

    for n in range(Z):
        if Y > 1:
            d = order(n)
            ya_copy(n).wait_recv()
            part_stack[d, 0:FIRST, y] = part_stack[d, 0:FIRST, y] + recv_ya[n]
        for g in range(FIRST):
            pass_on(n, g)
    finish(FIRST)
    if Y > 1:
        yb_copy().start()
    for g in range(FIRST):
        finish(g)
        start = SUB + band * g
        stack[start : start + band, 0:W] = part_stack[z, g, y]
    start = SUB + band * FIRST
    if Y > 1:
        yb_copy().wait_recv()
        stack[start : start + band, 0:W] = part_stack[z, FIRST, y] + recv_yb[...]
    else:
        stack[start : start + band, 0:W] = part_stack[z, FIRST, y]

    tap = tk.shape[0]
    weights = [[power(tk[a, 0, b]) for b in range(tap)] for a in range(tap)]
    for i in range(2 * R // SUB):
        def load(a):
            start = SUB * (i + 1) + a - tap // 2
            return stack[start : start + SUB, :]

        for k, piece in enumerate(filter_rows(load, weights, tap)):
            trail[SUB * i : SUB * (i + 1), LANES * k : LANES * (k + 1)] = piece

    end = pltpu.make_async_remote_copy(
        src_ref=trail.at[pl.ds(pl.multiple_of(R * (1 - c), SUB), R)],
        dst_ref=trail_in,
        send_sem=end_s,
        recv_sem=end_r,
        device_id=sky,
        device_id_type=MESH,
    )
    end.start()
    end.wait_recv()
    mine = trail[pl.ds(pl.multiple_of(R * c, SUB), R), :]
    theirs = trail_in[...]
    psi = jnp.where(c == 0, mine, theirs)
    phi = jnp.where(c == 0, theirs, mine)
    out[0] = psi / jnp.sqrt(phi + 1.0)

    for e in range(E):
        sky_copy(e).wait_send()
    end.wait_send()
    if Y > 1:
        yb_copy().wait_send()
        for n in range(Z):
            ya_copy(n).wait_send()
    for n in range(Z):
        d = order(n)

        @pl.when(d != z)
        def _():
            for g in range(FIRST + 1):
                line_copy(jnp.where(d > z, 0, 1), d, g).wait_send()


def shards(expo, science, inv_variance, pixel_masks, point_spread, tile_offset, column_shift, trail_kernel):
    E, R, W = science.shape
    Y = 2 if expo % 2 == 0 else 1
    Z = expo // Y
    band = R // 2
    taps = point_spread.shape[1]
    f32 = jnp.float32
    dma = pltpu.SemaphoreType.DMA
    hbm = pl.BlockSpec(memory_space=pl.ANY)
    return pl.pallas_call(
        functools.partial(kernel, (E, R, W, Y, Z)),
        out_shape=pltpu.VMEM((1, R, W), f32),
        in_specs=[hbm] * 7,
        out_specs=pl.BlockSpec(memory_space=pltpu.VMEM),
        scratch_shapes=[
            pltpu.SMEM((taps, E, taps), f32),
            pltpu.SMEM(tile_offset.shape[::-1], jnp.int32),
            pltpu.SMEM(column_shift.shape[::-1], jnp.int32),
            pltpu.SMEM((trail_kernel.shape[1], 1, trail_kernel.shape[2]), f32),
            pltpu.VMEM((E, R, W), f32),
            pltpu.VMEM((E, R, W), f32),
            pltpu.VMEM((E, R, W), jnp.int32),
            pltpu.VMEM((E, 2 * R + 2 * SUB, W), f32),
            pltpu.VMEM((E, R, W), f32),
            pltpu.VMEM((E, 2, W // LANES + 3, R, LANES), f32),
            pltpu.VMEM((Z, FIRST + 1, Y, band, W), f32),
            pltpu.VMEM((Z, FIRST, band, W), f32),
            pltpu.VMEM((band, W), f32),
            pltpu.VMEM((2, Z, FIRST, band, W), f32),
            pltpu.VMEM((2, Z, Y, band, W), f32),
            pltpu.VMEM((2 * R + 2 * SUB, W), f32),
            pltpu.VMEM((2 * R, W), f32),
            pltpu.VMEM((R, W), f32),
            dma((3, E)),
            dma((4,)),
            dma((E,)),
            dma((E,)),
            dma((Z,)),
            dma((Z,)),
            dma,
            dma,
            dma((2, Z, FIRST + 1)),
            dma((2, Z, FIRST + 1)),
            dma,
            dma,
        ],
        compiler_params=pltpu.CompilerParams(collective_id=0, has_side_effects=True),
    )(
        science,
        inv_variance,
        pixel_masks,
        jnp.transpose(point_spread, (1, 0, 2)),
        tile_offset.T,
        column_shift.T,
        jnp.transpose(trail_kernel, (1, 0, 2)),
    )


def solution(mesh):
    return jax.shard_map(
        functools.partial(shards, mesh.shape["expo"]),
        mesh=mesh,
        in_specs=(
            P(("field", "expo"), "sky", None),
            P(("field", "expo"), "sky", None),
            P(("field", "expo"), "sky", None),
            P(("field", "expo"), None, None),
            P(None, "expo"),
            P(None, "expo"),
            P("expo", None, None),
        ),
        out_specs=P(("field", "expo"), "sky", None),
        check_vma=False,
    )
```
